32 devices in a mesh: tm: 8 (over z, x), exp: 4 (over y, core).
Axes of the slice: x: 2, y: 2, z: 4, core: 2. Of those that a mesh axis runs over, the one named last changes fastest.
Arguments:
- transitions: float32 [512, 256, 256], P('tm'), may hold values from -0.2 to 1.2
- pattern: int32 [512, 4, 4], P('tm'), may hold values from 0 to 1, as said below
- obs_mask: int32 [4, 512, 256], P('exp', 'tm'), may hold values 0 or 1
- measured: float32 [4, 512, 256], P('exp', 'tm'), may hold values from -6 to 6
- prior_mean: float32 [4, 256], P('exp'), may hold values from -6 to 6
- filter_gain: float32 [256], replicated, may hold values from 0 to 0.6
- smooth_gain: float32 [256], replicated, may hold values from 0.3 to 1
Outputs:
- smoothed: float32 [4, 512, 256], P('exp', 'tm')
- information: float32 [256, 256], replicated
The draws below stay inside these ranges and needn't reach their ends.
Inputs may be any that keep to these rules, and one draw needn't show every extreme that they name: `pattern`: diagonal blocks are always present.
All inputs are finite; a program needn't handle non-finite values. No bound on the sum of `obs_mask` on one device may be relied on, other than what follows from the above.
Results may differ from the reference program's by a relative error of at most 0.0001.
Values sent between devices are 32-bit elements; how exact they have to be, the bound alone decides.
A program may use at most 192 MiB of HBM per device.

```python
import jax
import jax.numpy as jnp
from jax import lax

WIDTH = 256
BLOCK = 64
NBLK = 4
STEPS_DEV = 64
HORIZON_LENGTH = 512
EXPS = 4


def fast_size_bins(key):
    order = jax.random.permutation(jax.random.fold_in(key, 31), WIDTH)
    fast_count = WIDTH // 2
    return (order < fast_count).astype(jnp.float32)


def draw_transitions(key, part):
    fast = fast_size_bins(key)
    slow_rate = jax.random.uniform(jax.random.fold_in(key, 41), (WIDTH,), jnp.float32, 0.05, 0.5) / HORIZON_LENGTH
    fast_rate = 1.0 / (jax.random.uniform(jax.random.fold_in(key, 42), (WIDTH,), jnp.float32, 0.5, 0.8) * STEPS_DEV)
    enlargement_speed = fast * fast_rate + (1.0 - fast) * slow_rate
    block_total = HORIZON_LENGTH // STEPS_DEV
    block_scale = jnp.exp(jax.random.uniform(jax.random.fold_in(key, 43), (block_total,), jnp.float32, jnp.log(0.5), jnp.log(2.0)))
    multiplier_each_interval = jnp.repeat(block_scale, STEPS_DEV) * jax.random.uniform(jax.random.fold_in(key, 44), (HORIZON_LENGTH,), jnp.float32, 0.8, 1.2)
    spike_tally = jax.random.randint(jax.random.fold_in(key, 45), (HORIZON_LENGTH,), 0, HORIZON_LENGTH) < 3
    nucleation_spike = jnp.where(spike_tally, jax.random.uniform(jax.random.fold_in(key, 46), (HORIZON_LENGTH,), jnp.float32, 0.5, 0.8), 1.0)
    shrinkage_multiplier = jnp.exp(-multiplier_each_interval[:, None] * enlargement_speed[None, :]) * nucleation_spike[:, None]
    growth = jax.random.uniform(jax.random.fold_in(key, 47), (HORIZON_LENGTH,), jnp.float32, 1.0, 9.0) / HORIZON_LENGTH
    sigma = 1.0 / jnp.sqrt(jnp.float32(HORIZON_LENGTH * WIDTH))
    key_rand = jax.random.fold_in(key, 48)
    spread = jnp.clip(jax.random.normal(key_rand, (HORIZON_LENGTH, WIDTH, WIDTH), jnp.float32), -4.0, 4.0) * sigma
    identity = jnp.eye(WIDTH, dtype=jnp.float32)
    lower = jnp.eye(WIDTH, k=-1, dtype=jnp.float32)
    stay = shrinkage_multiplier * (1.0 - growth[:, None])
    move = shrinkage_multiplier * growth[:, None]
    result = spread + identity[None] * stay[:, None, :] + lower[None] * move[:, None, :]
    return result.astype(jnp.float32)


def draw_pattern(key, part):
    bits = jax.random.randint(jax.random.fold_in(key, 21), (HORIZON_LENGTH, NBLK, NBLK), 0, 2, jnp.int32)
    return jnp.maximum(bits, jnp.eye(NBLK, dtype=jnp.int32)[None])


def draw_filter_gain(key, part):
    fast = fast_size_bins(key)
    strong = jax.random.uniform(jax.random.fold_in(key, 51), (WIDTH,), jnp.float32, 0.15, 0.6)
    weak = jax.random.uniform(jax.random.fold_in(key, 52), (WIDTH,), jnp.float32, 0.1, 0.6) / HORIZON_LENGTH
    return (fast * strong + (1.0 - fast) * weak).astype(jnp.float32)


def draw_smooth_gain(key, part):
    fast = fast_size_bins(key)
    strong = jax.random.uniform(jax.random.fold_in(key, 61), (WIDTH,), jnp.float32, 0.3, 0.9)
    weak = 1.0 - jax.random.uniform(jax.random.fold_in(key, 62), (WIDTH,), jnp.float32, 0.05, 0.5) / HORIZON_LENGTH
    return (fast * strong + (1.0 - fast) * weak).astype(jnp.float32)


def with_ends(entries, key, least, top_value):
    spot = [jax.random.randint(jax.random.fold_in(key, axis), (), 0, length) for axis, length in enumerate(entries.shape)]
    longest = entries.shape.index(max(entries.shape))
    beside = spot[:longest] + [(spot[longest] + 1) % entries.shape[longest]] + spot[longest + 1:]
    return entries.at[tuple(spot)].set(least).at[tuple(beside)].set(top_value)


def level_of(own_key, dims, pieces, smallest, high):
    loudness, own = 1.0, jax.random.fold_in(own_key, 6)
    for axis_at, parts in pieces:
        steps = jnp.exp(jax.random.uniform(jax.random.fold_in(own, axis_at), (parts,), jnp.float32, smallest / len(pieces), high / len(pieces)))
        loudness = loudness * jnp.repeat(steps, dims[axis_at] // parts).reshape([-1 if axis == axis_at else 1 for axis in range(len(dims))])
    return loudness


def gaussian(rng, shape, scale, most, split=(), held_as=jnp.bfloat16):
    values = jax.random.normal(rng, shape, jnp.float32) * scale
    if len(split) > 0:
        values = level_of(rng, shape, split, -0.22, 0.18) * values
    return jnp.clip(values, min=-most, max=most).astype(held_as)


def setup_inputs(seed: int = 0) -> dict:
    splits = jax.random.split(jax.random.key(seed), 8)
    transitions = draw_transitions(jax.random.fold_in(splits[7], 71), 0)
    pattern = draw_pattern(jax.random.fold_in(splits[7], 71), 0)
    obs_mask = with_ends((jax.random.randint(splits[2], (EXPS, HORIZON_LENGTH, WIDTH), 0, 4) < 3).astype(jnp.int32), jax.random.fold_in(splits[2], 1), 0, 1)
    measured = gaussian(splits[3], (EXPS, HORIZON_LENGTH, WIDTH), 1.0, 6.0, ((0, 4), (1, 8)), jnp.float32)
    prior_mean = gaussian(splits[4], (EXPS, WIDTH), 1.0, 6.0, ((0, 4),), jnp.float32)
    filter_gain = draw_filter_gain(jax.random.fold_in(splits[7], 71), 0)
    smooth_gain = draw_smooth_gain(jax.random.fold_in(splits[7], 71), 0)
    return dict(transitions=transitions, pattern=pattern, obs_mask=obs_mask, measured=measured, prior_mean=prior_mean, filter_gain=filter_gain, smooth_gain=smooth_gain)


def dense_at(trans_step, pattern_step):
    reshaped = trans_step.astype(jnp.float32).reshape(NBLK, BLOCK, NBLK, BLOCK)
    weights = pattern_step.astype(jnp.float32)[:, None, :, None]
    return (reshaped * weights).reshape(WIDTH, WIDTH)


def reference(transitions, pattern, obs_mask, measured, prior_mean, filter_gain, smooth_gain):
    highest = lax.Precision.HIGHEST
    smooth_all = []
    total_info = jnp.zeros((WIDTH, WIDTH), jnp.float32)
    for experiment in range(EXPS):
        mask_rows = obs_mask[experiment].astype(jnp.float32)
        keep_rows = 1.0 - filter_gain[None, :] * mask_rows
        drive_terms = (filter_gain[None, :] * mask_rows) * measured[experiment].astype(jnp.float32)

        def forward(state, inputs):
            trans_step, pattern_step, keep_step, drive_step = inputs
            predict = jnp.dot(dense_at(trans_step, pattern_step), state, precision=highest)
            state = keep_step * predict + drive_step
            return state, (state, predict)

        last_state, (filtered, predicted) = lax.scan(forward, prior_mean[experiment], (transitions, pattern, keep_rows, drive_terms))

        def reversed_pass(carried, inputs):
            trans_step, pattern_step, state, predict = inputs
            smooth_now = state + smooth_gain * carried
            residual = smooth_now - predict
            carried = jnp.dot(residual, dense_at(trans_step, pattern_step), precision=highest)
            return carried, (smooth_now, residual)

        first_carry, (smoothed, residuals) = lax.scan(reversed_pass, jnp.zeros((WIDTH,), jnp.float32), (transitions, pattern, filtered, predicted), reverse=True)
        smooth_all.append(smoothed)
        total_info = total_info + jnp.dot(residuals.T, residuals, precision=highest)
    return jnp.stack(smooth_all), total_info / (EXPS * HORIZON_LENGTH)
```

```python
import functools

import jax
import jax.numpy as jnp
from jax import lax
from jax.experimental import pallas as pl
from jax.experimental.pallas import tpu as pltpu
from jax.sharding import PartitionSpec as P

HIGHEST = lax.Precision.HIGHEST
LANES = 128
SUB = 8
CHUNKS = 8
VMEM_BYTES = 60 * 1024 * 1024


def split(x):
    high = x.astype(jnp.bfloat16)
    low = (x - high.astype(jnp.float32)).astype(jnp.bfloat16)
    return high, low


def dot_rhs_t(a, b):
    return lax.dot_general(a, b, (((1,), (1,)), ((), ())), preferred_element_type=jnp.float32)


def to_column(row):
    width = row.shape[1]
    padded = jnp.concatenate([row, jnp.zeros((LANES - SUB, width), jnp.float32)], axis=0)
    return padded.T


def chain_kernel(pattern_ref, trans_ref, obs_ref, meas_ref, fgain_ref, sgain_ref,
                 dense_ref, apre_ref, bpre_ref, pmap_ref, ptot_ref, gain_ref, drive_ref, state, pre):
    j, c = pl.program_id(0), pl.program_id(1)
    length, chunks = pl.num_programs(0), pl.num_programs(1)
    t = c * length + j
    width = trans_ref.shape[-1]
    blocks = 4
    block = width // blocks
    lane = lax.broadcasted_iota(jnp.int32, (1, width), 1) // block
    pieces = []
    for i in range(blocks):
        weights = jnp.zeros((1, width), jnp.float32)
        for k in range(blocks):
            weights = jnp.where(lane == k, pattern_ref[t, i * blocks + k].astype(jnp.float32), weights)
        pieces.append(trans_ref[0, i * block:(i + 1) * block, :] * weights)
    dense = jnp.concatenate(pieces, axis=0)
    dense_ref[0] = dense
    fgain, sgain = fgain_ref[...], sgain_ref[...]
    gain = fgain * obs_ref[0, pl.ds(t, 1), :].astype(jnp.float32)
    keep = 1.0 - gain
    drive = gain * meas_ref[0, pl.ds(t, 1), :]
    gain_ref[j, pl.ds(c, 1), :] = gain
    drive_ref[j, pl.ds(c, 1), :] = drive

    @pl.when(j == 0)
    def _():
        turned = dense.T
        state[c, 0:width, :] = turned * keep
        state[c, width:2 * width, :] = turned * sgain
        state[c, 2 * width:, :] = jnp.broadcast_to(drive, (2 * SUB, width))

    @pl.when(j > 0)
    def _():
        rows = lax.broadcasted_iota(jnp.int32, (width, width), 0)
        cols = lax.broadcasted_iota(jnp.int32, (width, width), 1)
        on_diagonal = rows == cols
        diagonal = jnp.sum(jnp.where(on_diagonal, dense, 0.0), axis=0, keepdims=True)
        rest_high, rest_low = split(jnp.where(on_diagonal, 0.0, dense))
        now = state[c]
        high, low = split(now)
        new = now * diagonal + (
            dot_rhs_t(high, rest_high) + (dot_rhs_t(low, rest_high) + dot_rhs_t(high, rest_low))
        )
        state[c, 0:width, :] = new[0:width] * keep
        state[c, width:2 * width, :] = new[width:2 * width] * sgain
        state[c, 2 * width:, :] = new[2 * width:] * keep + drive

    @pl.when(j == length - 1)
    def _():
        pmap_ref[0] = state[c, width:2 * width, :]

        @pl.when(c == 0)
        def _():
            pre[...] = state[0]

        @pl.when(c > 0)
        def _():
            shift = state[c, 2 * width:, :]
            pre[0:width, :] = jnp.dot(pre[0:width, :], state[c, 0:width, :], precision=HIGHEST)
            pre[2 * width:, :] = jnp.dot(pre[2 * width:, :], state[c, 0:width, :], precision=HIGHEST) + shift
            pre[width:2 * width, :] = jnp.dot(
                pre[width:2 * width, :], state[c, width:2 * width, :], precision=HIGHEST)

        apre_ref[0] = pre[0:width, :]
        bpre_ref[0] = pre[2 * width:2 * width + SUB, :]

        @pl.when(c == chunks - 1)
        def _():
            ptot_ref[...] = pre[width:2 * width, :]


def chain(transitions, pattern, obs, meas, fgain, sgain):
    steps, width, _ = transitions.shape
    length = steps // CHUNKS
    at_end = lambda j, c, *_: (c * (j // (length - 1)), 0, 0)
    fixed = lambda j, c, *_: (0, 0)
    f32 = jnp.float32
    return pl.pallas_call(
        chain_kernel,
        grid_spec=pltpu.PrefetchScalarGridSpec(
            num_scalar_prefetch=1,
            grid=(length, CHUNKS),
            in_specs=[
                pl.BlockSpec((1, width, width), lambda j, c, *_: (c * length + j, 0, 0)),
                pl.BlockSpec((1, steps, width), lambda j, c, *_: (0, 0, 0)),
                pl.BlockSpec((1, steps, width), lambda j, c, *_: (0, 0, 0)),
                pl.BlockSpec((1, width), fixed),
                pl.BlockSpec((1, width), fixed),
            ],
            out_specs=[
                pl.BlockSpec((1, width, width), lambda j, c, *_: (c * length + j, 0, 0)),
                pl.BlockSpec((1, width, width), at_end),
                pl.BlockSpec((1, SUB, width), at_end),
                pl.BlockSpec((1, width, width), at_end),
                pl.BlockSpec((width, width), fixed),
                pl.BlockSpec((length, CHUNKS, width), lambda *_: (0, 0, 0)),
                pl.BlockSpec((length, CHUNKS, width), lambda *_: (0, 0, 0)),
            ],
            scratch_shapes=[
                pltpu.VMEM((CHUNKS, 2 * width + 2 * SUB, width), f32),
                pltpu.VMEM((2 * width + 2 * SUB, width), f32),
            ],
        ),
        out_shape=[
            jax.ShapeDtypeStruct((steps, width, width), f32),
            jax.ShapeDtypeStruct((CHUNKS, width, width), f32),
            jax.ShapeDtypeStruct((CHUNKS, SUB, width), f32),
            jax.ShapeDtypeStruct((CHUNKS, width, width), f32),
            jax.ShapeDtypeStruct((width, width), f32),
            jax.ShapeDtypeStruct((length, CHUNKS, width), f32),
            jax.ShapeDtypeStruct((length, CHUNKS, width), f32),
        ],
        compiler_params=pltpu.CompilerParams(vmem_limit_bytes=VMEM_BYTES),
    )(pattern, transitions, obs, meas, fgain, sgain)


def relay_kernel(count, reverse, map_ref, shift_ref, first_ref, out_ref, inbox, outbox, send_sem, recv_sem):
    me = lax.axis_index("tm")
    place = count - 1 - me if reverse else me
    step = -1 if reverse else 1
    barrier = pltpu.get_barrier_semaphore()

    @pl.when(place > 0)
    def _():
        pl.semaphore_signal(barrier, inc=1, device_id={"tm": me - step})

    @pl.when(place < count - 1)
    def _():
        pl.semaphore_signal(barrier, inc=1, device_id={"tm": me + step})

    ends = (place == 0) | (place == count - 1)

    @pl.when(ends)
    def _():
        pl.semaphore_wait(barrier, 1)

    @pl.when(jnp.logical_not(ends))
    def _():
        pl.semaphore_wait(barrier, 2)

    arrow = functools.partial(
        pltpu.make_async_remote_copy, src_ref=outbox, dst_ref=inbox, send_sem=send_sem, recv_sem=recv_sem)

    @pl.when(place > 0)
    def _():
        arrow(device_id={"tm": me - step}).wait_recv()
        out_ref[...] = inbox[...]

    @pl.when(place == 0)
    def _():
        out_ref[...] = first_ref[...]

    @pl.when(place < count - 1)
    def _():
        entering = out_ref[...]
        if reverse:
            moved = jnp.sum(map_ref[...] * entering[0:1], axis=1, keepdims=True)
            row = jnp.broadcast_to(moved, (moved.shape[0], LANES)).T[0:SUB]
        else:
            column = to_column(entering)[:, 0:1]
            row = jnp.broadcast_to(
                jnp.sum(map_ref[...] * column, axis=0, keepdims=True), entering.shape)
        outbox[...] = row + shift_ref[...]
        going = arrow(device_id={"tm": me + step})
        going.start()
        going.wait_send()


def relay(maps, shift, first, reverse, ident):
    count = lax.axis_size("tm")
    width = first.shape[1]
    whole = pl.BlockSpec((SUB, width), lambda i: (0, 0))
    last = maps.shape[0] - 1 if maps.ndim == 3 else 0
    map_spec = (pl.BlockSpec((None, width, width), lambda i: (last, 0, 0)) if maps.ndim == 3
                else pl.BlockSpec((width, width), lambda i: (0, 0)))
    shift_spec = (pl.BlockSpec((None, SUB, width), lambda i: (last, 0, 0)) if shift.ndim == 3 else whole)
    return pl.pallas_call(
        functools.partial(relay_kernel, count, reverse),
        grid=(1,),
        in_specs=[map_spec, shift_spec, whole],
        out_specs=whole,
        out_shape=jax.ShapeDtypeStruct((SUB, width), jnp.float32),
        scratch_shapes=[
            pltpu.VMEM((SUB, width), jnp.float32),
            pltpu.VMEM((SUB, width), jnp.float32),
            pltpu.SemaphoreType.DMA,
            pltpu.SemaphoreType.DMA,
        ],
        compiler_params=pltpu.CompilerParams(collective_id=ident, has_side_effects=True),
    )(maps, shift, first)


def turned_step(dense_ref, j, values):
    columns = to_column(values)
    rows = [
        jnp.sum(dense_ref[c, j] * columns[:, c:c + 1], axis=0, keepdims=True) for c in range(CHUNKS)
    ]
    return jnp.concatenate(rows, axis=0)


def filter_kernel(dense_ref, apre_ref, bpre_ref, pmap_ref, start_ref, gain_ref, drive_ref, sgain_ref,
                  filtered_ref, change_ref, carried_ref, shift_ref):
    chunks, length, width, _ = dense_ref.shape
    column = to_column(start_ref[...])[:, 0:1]
    rows = [start_ref[0:1, :]]
    for c in range(chunks - 1):
        rows.append(bpre_ref[c, 0:1, :] + jnp.sum(apre_ref[c] * column, axis=0, keepdims=True))
    start = jnp.concatenate(rows, axis=0)
    lane = lax.broadcasted_iota(jnp.int32, (width, LANES), 1)

    def forward(j, state):
        gathered = jnp.zeros((width, LANES), jnp.float32)
        for c in range(chunks):
            moved = jnp.sum(dense_ref[c, j] * state[c:c + 1, :], axis=1, keepdims=True)
            gathered = jnp.where(lane == c, moved, gathered)
        predict = gathered.T[0:chunks]
        new = (1.0 - gain_ref[j]) * predict + drive_ref[j]
        filtered_ref[j] = new
        change_ref[j] = new - predict
        return new

    lax.fori_loop(0, length, forward, start)

    def backward(i, carried):
        j = length - 1 - i
        return turned_step(dense_ref, j, change_ref[j] + sgain_ref[...] * carried)

    carried = lax.fori_loop(0, length, backward, jnp.zeros((chunks, width), jnp.float32))
    carried_ref[...] = carried
    total = carried[chunks - 1:chunks]
    for c in range(chunks - 2, -1, -1):
        moved = jnp.sum(pmap_ref[c] * total, axis=1, keepdims=True)
        total = carried[c:c + 1] + jnp.broadcast_to(moved, (width, LANES)).T[0:1]
    shift_ref[...] = jnp.broadcast_to(total, (SUB, width))


def smoother_kernel(dense_ref, pmap_ref, enter_ref, carried_ref, filtered_ref, change_ref, sgain_ref,
                    smoothed_ref, info_ref, residuals):
    chunks, length, width, _ = dense_ref.shape
    carried = carried_ref[...]
    rows = [enter_ref[0:1, :]]
    for c in range(chunks - 1, 0, -1):
        moved = jnp.sum(pmap_ref[c] * rows[0], axis=1, keepdims=True)
        rows.insert(0, carried[c:c + 1] + jnp.broadcast_to(moved, (width, LANES)).T[0:1])
    start = jnp.concatenate(rows, axis=0)

    def backward(i, carry):
        j = length - 1 - i
        lifted = sgain_ref[...] * carry
        smoothed = filtered_ref[j] + lifted
        for c in range(chunks):
            smoothed_ref[0, pl.ds(c * length + j, 1), :] = smoothed[c:c + 1]
        residual = change_ref[j] + lifted
        residuals[j] = residual
        return turned_step(dense_ref, j, residual)

    lax.fori_loop(0, length, backward, start)
    every = residuals[...].reshape(length * chunks, width)
    info_ref[...] = lax.dot_general(
        every, every, (((0,), (0,)), ((), ())), precision=HIGHEST, preferred_element_type=jnp.float32)


def shards(transitions, pattern, obs_mask, measured, prior_mean, filter_gain, smooth_gain):
    steps, width, _ = transitions.shape
    length = steps // CHUNKS
    f32 = jnp.float32
    fgain, sgain = filter_gain[None, :], smooth_gain[None, :]
    dense, apre, bpre, pmap, ptot, gain, drive = chain(
        transitions, pattern.reshape(steps, -1), obs_mask, measured, fgain, sgain)
    dense = dense.reshape(CHUNKS, length, width, width)
    first = jnp.broadcast_to(prior_mean, (SUB, width))
    start = relay(apre, bpre, first, False, 0)
    per_step = jax.ShapeDtypeStruct((length, CHUNKS, width), f32)
    row = jax.ShapeDtypeStruct((SUB, width), f32)
    params = pltpu.CompilerParams(vmem_limit_bytes=VMEM_BYTES)
    vmem = pl.BlockSpec(memory_space=pltpu.VMEM)
    filtered, change, carried, shift = pl.pallas_call(
        filter_kernel,
        in_specs=[vmem] * 8,
        out_specs=[vmem] * 4,
        out_shape=[per_step, per_step, row, row],
        compiler_params=params,
    )(dense, apre, bpre, pmap, start, gain, drive, sgain)
    entering = relay(ptot, shift, jnp.zeros((SUB, width), f32), True, 1)
    smoothed, local_info = pl.pallas_call(
        smoother_kernel,
        in_specs=[vmem] * 7,
        out_specs=[vmem] * 2,
        out_shape=[jax.ShapeDtypeStruct((1, steps, width), f32), jax.ShapeDtypeStruct((width, width), f32)],
        scratch_shapes=[pltpu.VMEM((length, CHUNKS, width), f32)],
        compiler_params=params,
    )(dense, pmap, entering, carried, filtered, change, sgain)
    total_info = lax.psum(local_info, ("tm", "exp"))
    information = total_info / (steps * lax.axis_size("tm") * lax.axis_size("exp"))
    return smoothed, information


def solution(mesh):
    in_specs = (
        P("tm", None, None),
        P("tm", None, None),
        P("exp", "tm", None),
        P("exp", "tm", None),
        P("exp", None),
        P(),
        P(),
    )
    out_specs = (P("exp", "tm", None), P())
    return jax.shard_map(shards, mesh=mesh, in_specs=in_specs, out_specs=out_specs, check_vma=False)
```

```python
import functools

import jax
import jax.numpy as jnp
from jax import lax
from jax.experimental import pallas as pl
from jax.experimental.pallas import tpu as pltpu
from jax.sharding import PartitionSpec as P

HIGHEST = lax.Precision.HIGHEST
LANES = 128
SUB = 8
CHUNKS = 8
VMEM_BYTES = 60 * 1024 * 1024


def split(x):
    high = x.astype(jnp.bfloat16)
    low = (x - high.astype(jnp.float32)).astype(jnp.bfloat16)
    return high, low


def dot_rhs_t(a, b):
    return lax.dot_general(a, b, (((1,), (1,)), ((), ())), preferred_element_type=jnp.float32)


def to_column(row):
    width = row.shape[1]
    padded = jnp.concatenate([row, jnp.zeros((LANES - SUB, width), jnp.float32)], axis=0)
    return padded.T


def chain_kernel(pattern_ref, trans_ref, obs_ref, meas_ref, fgain_ref, sgain_ref,
                 dense_ref, apre_ref, bpre_ref, pmap_ref, ptot_ref, gain_ref, drive_ref, state, pre):
    j, c = pl.program_id(0), pl.program_id(1)
    length, chunks = pl.num_programs(0), pl.num_programs(1)
    t = c * length + j
    width = trans_ref.shape[-1]
    blocks = 4
    block = width // blocks
    lane = lax.broadcasted_iota(jnp.int32, (1, width), 1) // block
    pieces = []
    for i in range(blocks):
        weights = jnp.zeros((1, width), jnp.float32)
        for k in range(blocks):
            weights = jnp.where(lane == k, pattern_ref[t, i * blocks + k].astype(jnp.float32), weights)
        pieces.append(trans_ref[0, i * block:(i + 1) * block, :] * weights)
    dense = jnp.concatenate(pieces, axis=0)
    dense_ref[0] = dense
    fgain, sgain = fgain_ref[...], sgain_ref[...]
    gain = fgain * obs_ref[0, pl.ds(t, 1), :].astype(jnp.float32)
    keep = 1.0 - gain
    drive = gain * meas_ref[0, pl.ds(t, 1), :]
    gain_ref[j, pl.ds(c, 1), :] = gain
    drive_ref[j, pl.ds(c, 1), :] = drive

    @pl.when(j == 0)
    def _():
        turned = dense.T
        state[c, 0:width, :] = turned * keep
        state[c, width:2 * width, :] = turned * sgain
        state[c, 2 * width:, :] = jnp.broadcast_to(drive, (2 * SUB, width))

    @pl.when(j > 0)
    def _():
        rows = lax.broadcasted_iota(jnp.int32, (width, width), 0)
        cols = lax.broadcasted_iota(jnp.int32, (width, width), 1)
        on_diagonal = rows == cols
        diagonal = jnp.sum(jnp.where(on_diagonal, dense, 0.0), axis=0, keepdims=True)
        rest_high, rest_low = split(jnp.where(on_diagonal, 0.0, dense))
        now = state[c]
        high, low = split(now)
        new = now * diagonal + (
            dot_rhs_t(high, rest_high) + (dot_rhs_t(low, rest_high) + dot_rhs_t(high, rest_low))
        )
        state[c, 0:width, :] = new[0:width] * keep
        state[c, width:2 * width, :] = new[width:2 * width] * sgain
        state[c, 2 * width:, :] = new[2 * width:] * keep + drive

    @pl.when(j == length - 1)
    def _():
        pmap_ref[0] = state[c, width:2 * width, :]

        @pl.when(c == 0)
        def _():
            pre[...] = state[0]

        @pl.when(c > 0)
        def _():
            shift = state[c, 2 * width:, :]
            pre[0:width, :] = jnp.dot(pre[0:width, :], state[c, 0:width, :], precision=HIGHEST)
            pre[2 * width:, :] = jnp.dot(pre[2 * width:, :], state[c, 0:width, :], precision=HIGHEST) + shift
            pre[width:2 * width, :] = jnp.dot(
                pre[width:2 * width, :], state[c, width:2 * width, :], precision=HIGHEST)

        apre_ref[0] = pre[0:width, :]
        bpre_ref[0] = pre[2 * width:2 * width + SUB, :]

        @pl.when(c == chunks - 1)
        def _():
            ptot_ref[...] = pre[width:2 * width, :]


def chain(transitions, pattern, obs, meas, fgain, sgain):
    steps, width, _ = transitions.shape
    length = steps // CHUNKS
    at_end = lambda j, c, *_: (c * (j // (length - 1)), 0, 0)
    fixed = lambda j, c, *_: (0, 0)
    f32 = jnp.float32
    return pl.pallas_call(
        chain_kernel,
        grid_spec=pltpu.PrefetchScalarGridSpec(
            num_scalar_prefetch=1,
            grid=(length, CHUNKS),
            in_specs=[
                pl.BlockSpec((1, width, width), lambda j, c, *_: (c * length + j, 0, 0)),
                pl.BlockSpec((1, steps, width), lambda j, c, *_: (0, 0, 0)),
                pl.BlockSpec((1, steps, width), lambda j, c, *_: (0, 0, 0)),
                pl.BlockSpec((1, width), fixed),
                pl.BlockSpec((1, width), fixed),
            ],
            out_specs=[
                pl.BlockSpec((1, width, width), lambda j, c, *_: (c * length + j, 0, 0)),
                pl.BlockSpec((1, width, width), at_end),
                pl.BlockSpec((1, SUB, width), at_end),
                pl.BlockSpec((1, width, width), at_end),
                pl.BlockSpec((width, width), fixed),
                pl.BlockSpec((length, CHUNKS, width), lambda *_: (0, 0, 0)),
                pl.BlockSpec((length, CHUNKS, width), lambda *_: (0, 0, 0)),
            ],
            scratch_shapes=[
                pltpu.VMEM((CHUNKS, 2 * width + 2 * SUB, width), f32),
                pltpu.VMEM((2 * width + 2 * SUB, width), f32),
            ],
        ),
        out_shape=[
            jax.ShapeDtypeStruct((steps, width, width), f32),
            jax.ShapeDtypeStruct((CHUNKS, width, width), f32),
            jax.ShapeDtypeStruct((CHUNKS, SUB, width), f32),
            jax.ShapeDtypeStruct((CHUNKS, width, width), f32),
            jax.ShapeDtypeStruct((width, width), f32),
            jax.ShapeDtypeStruct((length, CHUNKS, width), f32),
            jax.ShapeDtypeStruct((length, CHUNKS, width), f32),
        ],
        compiler_params=pltpu.CompilerParams(vmem_limit_bytes=VMEM_BYTES),
    )(pattern, transitions, obs, meas, fgain, sgain)


def relay_kernel(count, reverse, map_ref, shift_ref, first_ref, out_ref, inbox, outbox, send_sem, recv_sem):
    me = lax.axis_index("tm")
    place = count - 1 - me if reverse else me
    step = -1 if reverse else 1
    barrier = pltpu.get_barrier_semaphore()

    @pl.when(place > 0)
    def _():
        pl.semaphore_signal(barrier, inc=1, device_id={"tm": me - step})

    @pl.when(place < count - 1)
    def _():
        pl.semaphore_signal(barrier, inc=1, device_id={"tm": me + step})

    ends = (place == 0) | (place == count - 1)

    @pl.when(ends)
    def _():
        pl.semaphore_wait(barrier, 1)

    @pl.when(jnp.logical_not(ends))
    def _():
        pl.semaphore_wait(barrier, 2)

    arrow = functools.partial(
        pltpu.make_async_remote_copy, src_ref=outbox, dst_ref=inbox, send_sem=send_sem, recv_sem=recv_sem)

    @pl.when(place > 0)
    def _():
        arrow(device_id={"tm": me - step}).wait_recv()
        out_ref[...] = inbox[...]

    @pl.when(place == 0)
    def _():
        out_ref[...] = first_ref[...]

    @pl.when(place < count - 1)
    def _():
        entering = out_ref[...]
        if reverse:
            moved = jnp.sum(map_ref[...] * entering[0:1], axis=1, keepdims=True)
            row = jnp.broadcast_to(moved, (moved.shape[0], LANES)).T[0:SUB]
        else:
            column = to_column(entering)[:, 0:1]
            row = jnp.broadcast_to(
                jnp.sum(map_ref[...] * column, axis=0, keepdims=True), entering.shape)
        outbox[...] = row + shift_ref[...]
        going = arrow(device_id={"tm": me + step})
        going.start()
        going.wait_send()


def relay(maps, shift, first, reverse, ident):
    count = lax.axis_size("tm")
    width = first.shape[1]
    whole = pl.BlockSpec((SUB, width), lambda i: (0, 0))
    last = maps.shape[0] - 1 if maps.ndim == 3 else 0
    map_spec = (pl.BlockSpec((None, width, width), lambda i: (last, 0, 0)) if maps.ndim == 3
                else pl.BlockSpec((width, width), lambda i: (0, 0)))
    shift_spec = (pl.BlockSpec((None, SUB, width), lambda i: (last, 0, 0)) if shift.ndim == 3 else whole)
    return pl.pallas_call(
        functools.partial(relay_kernel, count, reverse),
        grid=(1,),
        in_specs=[map_spec, shift_spec, whole],
        out_specs=whole,
        out_shape=jax.ShapeDtypeStruct((SUB, width), jnp.float32),
        scratch_shapes=[
            pltpu.VMEM((SUB, width), jnp.float32),
            pltpu.VMEM((SUB, width), jnp.float32),
            pltpu.SemaphoreType.DMA,
            pltpu.SemaphoreType.DMA,
        ],
        compiler_params=pltpu.CompilerParams(collective_id=ident, has_side_effects=True),
    )(maps, shift, first)


def turned_step(dense_ref, values):
    columns = to_column(values)
    rows = [
        jnp.sum(dense_ref[c] * columns[:, c:c + 1], axis=0, keepdims=True) for c in range(CHUNKS)
    ]
    return jnp.concatenate(rows, axis=0)


def filter_kernel(dense_ref, apre_ref, bpre_ref, pmap_ref, start_ref, gain_ref, drive_ref, sgain_ref,
                  filtered_ref, change_ref, carried_ref, shift_ref, state):
    i, length = pl.program_id(0), filtered_ref.shape[0]
    chunks, width, _ = dense_ref.shape

    @pl.when(i == 0)
    def _():
        column = to_column(start_ref[...])[:, 0:1]
        rows = [start_ref[0:1, :]]
        for c in range(chunks - 1):
            rows.append(bpre_ref[c, 0:1, :] + jnp.sum(apre_ref[c] * column, axis=0, keepdims=True))
        state[...] = jnp.concatenate(rows, axis=0)

    @pl.when(i < length)
    def _():
        lane = lax.broadcasted_iota(jnp.int32, (width, LANES), 1)
        gathered = jnp.zeros((width, LANES), jnp.float32)
        for c in range(chunks):
            moved = jnp.sum(dense_ref[c] * state[c:c + 1, :], axis=1, keepdims=True)
            gathered = jnp.where(lane == c, moved, gathered)
        predict = gathered.T[0:chunks]
        new = (1.0 - gain_ref[i]) * predict + drive_ref[i]
        filtered_ref[i] = new
        change_ref[i] = new - predict
        state[...] = new

    @pl.when(i == length)
    def _():
        state[...] = jnp.zeros_like(state)

    @pl.when(i >= length)
    def _():
        j = 2 * length - 1 - i
        state[...] = turned_step(dense_ref, change_ref[j] + sgain_ref[...] * state[...])

    @pl.when(i == 2 * length - 1)
    def _():
        carried = state[...]
        carried_ref[...] = carried
        total = carried[chunks - 1:chunks]
        for c in range(chunks - 2, -1, -1):
            moved = jnp.sum(pmap_ref[c] * total, axis=1, keepdims=True)
            total = carried[c:c + 1] + jnp.broadcast_to(moved, (width, LANES)).T[0:1]
        shift_ref[...] = jnp.broadcast_to(total, (SUB, width))


def smoother_kernel(dense_ref, pmap_ref, enter_ref, carried_ref, filtered_ref, change_ref, sgain_ref,
                    smoothed_ref, info_ref, residuals, state):
    i, length = pl.program_id(0), filtered_ref.shape[0]
    chunks, width, _ = dense_ref.shape

    @pl.when(i == 0)
    def _():
        carried = carried_ref[...]
        rows = [enter_ref[0:1, :]]
        for c in range(chunks - 1, 0, -1):
            moved = jnp.sum(pmap_ref[c] * rows[0], axis=1, keepdims=True)
            rows.insert(0, carried[c:c + 1] + jnp.broadcast_to(moved, (width, LANES)).T[0:1])
        state[...] = jnp.concatenate(rows, axis=0)

    j = length - 1 - i
    lifted = sgain_ref[...] * state[...]
    smoothed = filtered_ref[j] + lifted
    for c in range(chunks):
        smoothed_ref[0, pl.ds(c * length + j, 1), :] = smoothed[c:c + 1]
    residual = change_ref[j] + lifted
    residuals[j] = residual

    @pl.when(i < length - 1)
    def _():
        state[...] = turned_step(dense_ref, residual)

    @pl.when(i == length - 1)
    def _():
        every = residuals[...].reshape(length * chunks, width)
        info_ref[...] = lax.dot_general(
            every, every, (((0,), (0,)), ((), ())), precision=HIGHEST, preferred_element_type=jnp.float32)


def total_kernel(parts, blocks, scale, local_ref, out_ref, part, box_e, box_t, send_sem, recv_sem):
    e, t = lax.axis_index("exp"), lax.axis_index("tm")
    barrier = pltpu.get_barrier_semaphore()
    e_peers = [lax.rem(e + k, parts) for k in range(1, parts)]
    t_peers = [lax.rem(t + k, blocks) for k in range(1, blocks)]
    for peer in e_peers:
        pl.semaphore_signal(barrier, inc=1, device_id={"exp": peer})
    for peer in t_peers:
        pl.semaphore_signal(barrier, inc=1, device_id={"tm": peer})
    pl.semaphore_wait(barrier, parts + blocks - 2)

    def send(src, dst, number, device):
        copy = pltpu.make_async_remote_copy(
            src_ref=src, dst_ref=dst, send_sem=send_sem.at[number], recv_sem=recv_sem.at[number],
            device_id=device)
        copy.start()
        return copy

    first = [send(local_ref.at[p], box_e.at[k], k, {"exp": p}) for k, p in enumerate(e_peers)]
    base = len(first)
    value = local_ref[e]
    for k, copy in enumerate(first):
        copy.wait_recv()
        value = value + box_e[k]
    part[...] = value
    second = [send(part.at[p], box_t.at[k], base + k, {"tm": p}) for k, p in enumerate(t_peers)]
    base += len(second)
    mine = part[t]
    for k, copy in enumerate(second):
        copy.wait_recv()
        mine = mine + box_t[k]
    out_ref[e, t] = mine * scale
    third = [send(out_ref.at[e, t], out_ref.at[e, t], base + k, {"tm": p}) for k, p in enumerate(t_peers)]
    base += len(third)
    for k, copy in enumerate(third):
        sender = lax.rem(t + blocks - 1 - k, blocks)
        pltpu.make_async_remote_copy(
            src_ref=out_ref.at[e, sender], dst_ref=out_ref.at[e, sender], send_sem=send_sem.at[base - len(third) + k],
            recv_sem=recv_sem.at[base - len(third) + k], device_id={"tm": sender}).wait_recv()
    fourth = [send(out_ref.at[e], out_ref.at[e], base + k, {"exp": p}) for k, p in enumerate(e_peers)]
    for k, copy in enumerate(fourth):
        sender = lax.rem(e + parts - 1 - k, parts)
        pltpu.make_async_remote_copy(
            src_ref=out_ref.at[sender], dst_ref=out_ref.at[sender], send_sem=send_sem.at[base + k],
            recv_sem=recv_sem.at[base + k], device_id={"exp": sender}).wait_recv()
    for copy in first + second + third + fourth:
        copy.wait_send()


def total(local, scale, ident):
    parts, blocks = lax.axis_size("exp"), lax.axis_size("tm")
    width = local.shape[0]
    rows = width // (parts * blocks)
    copies = 2 * (parts - 1) + 2 * (blocks - 1)
    f32 = jnp.float32
    vmem = pl.BlockSpec(memory_space=pltpu.VMEM)
    summed = pl.pallas_call(
        functools.partial(total_kernel, parts, blocks, scale),
        in_specs=[vmem],
        out_specs=vmem,
        out_shape=jax.ShapeDtypeStruct((parts, blocks, rows, width), f32),
        scratch_shapes=[
            pltpu.VMEM((blocks, rows, width), f32),
            pltpu.VMEM((parts - 1, blocks, rows, width), f32),
            pltpu.VMEM((blocks - 1, rows, width), f32),
            pltpu.SemaphoreType.DMA((copies,)),
            pltpu.SemaphoreType.DMA((copies,)),
        ],
        compiler_params=pltpu.CompilerParams(collective_id=ident, has_side_effects=True),
    )(local.reshape(parts, blocks, rows, width))
    return summed.reshape(width, width)


def shards(transitions, pattern, obs_mask, measured, prior_mean, filter_gain, smooth_gain):
    steps, width, _ = transitions.shape
    length = steps // CHUNKS
    f32 = jnp.float32
    fgain, sgain = filter_gain[None, :], smooth_gain[None, :]
    dense, apre, bpre, pmap, ptot, gain, drive = chain(
        transitions, pattern.reshape(steps, -1), obs_mask, measured, fgain, sgain)
    dense = dense.reshape(CHUNKS, length, width, width)
    first = jnp.broadcast_to(prior_mean, (SUB, width))
    start = relay(apre, bpre, first, False, 0)
    per_step = jax.ShapeDtypeStruct((length, CHUNKS, width), f32)
    row = jax.ShapeDtypeStruct((SUB, width), f32)
    params = pltpu.CompilerParams(vmem_limit_bytes=VMEM_BYTES)
    fixed = lambda array: pl.BlockSpec(array.shape, lambda i: (0,) * len(array.shape))
    moving = lambda at: pl.BlockSpec((CHUNKS, None, width, width), lambda i: (0, at(i), 0, 0))
    others = (apre, bpre, pmap, start, gain, drive, sgain)
    filtered, change, carried, shift = pl.pallas_call(
        filter_kernel,
        grid=(2 * length,),
        in_specs=[moving(lambda i: jnp.minimum(i, 2 * length - 1 - i))] + [fixed(x) for x in others],
        out_specs=[fixed(x) for x in (per_step, per_step, row, row)],
        out_shape=[per_step, per_step, row, row],
        scratch_shapes=[pltpu.VMEM((CHUNKS, width), f32)],
        compiler_params=params,
    )(dense, *others)
    entering = relay(ptot, shift, jnp.zeros((SUB, width), f32), True, 1)
    others = (pmap, entering, carried, filtered, change, sgain)
    outs = [jax.ShapeDtypeStruct((1, steps, width), f32), jax.ShapeDtypeStruct((width, width), f32)]
    smoothed, local_info = pl.pallas_call(
        smoother_kernel,
        grid=(length,),
        in_specs=[moving(lambda i: length - 1 - i)] + [fixed(x) for x in others],
        out_specs=[fixed(x) for x in outs],
        out_shape=outs,
        scratch_shapes=[pltpu.VMEM((length, CHUNKS, width), f32), pltpu.VMEM((CHUNKS, width), f32)],
        compiler_params=params,
    )(dense, *others)
    scale = 1.0 / (steps * lax.axis_size("tm") * lax.axis_size("exp"))
    information = total(local_info, scale, 2)
    return smoothed, information


def solution(mesh):
    in_specs = (
        P("tm", None, None),
        P("tm", None, None),
        P("exp", "tm", None),
        P("exp", "tm", None),
        P("exp", None),
        P(),
        P(),
    )
    out_specs = (P("exp", "tm", None), P())
    return jax.shard_map(shards, mesh=mesh, in_specs=in_specs, out_specs=out_specs, check_vma=False)
```

```python
import functools

import jax
import jax.numpy as jnp
from jax import lax
from jax.experimental import pallas as pl
from jax.experimental.pallas import tpu as pltpu
from jax.sharding import PartitionSpec as P

HIGHEST = lax.Precision.HIGHEST
LANES = 128
SUB = 8
CHUNKS = 8
GROUP = 2
PACE = 16
VMEM_BYTES = 60 * 1024 * 1024


def split(x):
    high = x.astype(jnp.bfloat16)
    low = (x - high.astype(jnp.float32)).astype(jnp.bfloat16)
    return high, low


def dot_rhs_t(a, b):
    return lax.dot_general(a, b, (((1,), (1,)), ((), ())), preferred_element_type=jnp.float32)


def to_column(row):
    width = row.shape[1]
    padded = jnp.concatenate([row, jnp.zeros((LANES - SUB, width), jnp.float32)], axis=0)
    return padded.T


def estimate_kernel(count, pace, pattern_ref, trans_ref, obs_ref, meas_ref, fgain_ref, sgain_ref, prior_ref,
                    smoothed_ref, info_ref,
                    dense, rest_high, rest_low, diagonals, gains, drives, fmaps, shifts, smaps, prefix, prefix_shift,
                    filtered, change, out_f, in_f, out_s, in_s, load_sem, send_sem, recv_sem):
    me = lax.axis_index("tm")
    chunks, length, width, _ = dense.shape
    blocks = pattern_ref.shape[1]
    block = width // blocks
    groups = chunks // GROUP
    f32 = jnp.float32
    barrier = pltpu.get_barrier_semaphore()

    @pl.when(me > 0)
    def _():
        pl.semaphore_signal(barrier, inc=1, device_id={"tm": me - 1})

    @pl.when(me < count - 1)
    def _():
        pl.semaphore_signal(barrier, inc=1, device_id={"tm": me + 1})

    def load(j):
        return pltpu.make_async_copy(trans_ref.at[:, j], dense.at[:, j], load_sem.at[j])

    for j in range(length):
        load(j).start()
    fgain, sgain = fgain_ref[...], sgain_ref[...]
    lane = lax.broadcasted_iota(jnp.int32, (1, width), 1) // block
    on_diagonal = (lax.broadcasted_iota(jnp.int32, (width, width), 0)
                   == lax.broadcasted_iota(jnp.int32, (width, width), 1))

    def gains_of(c, j):
        t = c * length + j
        gain = fgain * obs_ref[0, pl.ds(t, 1), :].astype(f32)
        drive = gain * meas_ref[0, pl.ds(t, 1), :]
        gains[j, pl.ds(c, 1), :] = gain
        drives[j, pl.ds(c, 1), :] = drive
        return 1.0 - gain, drive

    def masked(c, j):
        t = c * length + j
        pieces = []
        for i in range(blocks):
            weights = jnp.zeros((1, width), f32)
            for k in range(blocks):
                weights = jnp.where(lane == k, pattern_ref[t, i, k].astype(f32), weights)
            pieces.append(dense[c, j, i * block:(i + 1) * block, :] * weights)
        value = jnp.concatenate(pieces, axis=0)
        dense[c, j] = value
        return value

    def propagate(rows, diagonal, right_high, right_low):
        high, low = split(rows)
        left = jnp.concatenate([high, low, high], axis=1)
        right = jnp.concatenate([right_high, right_high, right_low], axis=1)
        return rows * diagonal + dot_rhs_t(left, right)

    load(0).wait()

    def first_step(c, _):
        keep, drive = gains_of(c, 0)
        turned = masked(c, 0).T
        fmaps[c] = turned * keep
        smaps[c] = turned * sgain
        shifts[c] = jnp.broadcast_to(drive, (2 * SUB, width))
        return 0

    lax.fori_loop(0, chunks, first_step, 0)

    def filter_step(j, _):
        load(j).wait()

        def group_step(g, _):
            for k in range(GROUP):
                c = g * GROUP + k
                keep, drive = gains_of(c, j)
                value = masked(c, j)
                diagonal = jnp.sum(jnp.where(on_diagonal, value, 0.0), axis=0, keepdims=True)
                high, low = split(jnp.where(on_diagonal, 0.0, value))
                diagonals[c, pl.ds(j, 1), :] = diagonal
                rest_high[c, j] = high
                rest_low[c, j] = low
                moved = propagate(jnp.concatenate([fmaps[c], shifts[c]], axis=0), diagonal, high, low)
                fmaps[c] = moved[0:width] * keep
                shifts[c] = moved[width:] * keep + drive
            return 0

        return lax.fori_loop(0, groups, group_step, 0)

    lax.fori_loop(1, length, filter_step, 0)

    prefix[0] = fmaps[0]
    prefix_shift[0] = shifts[0]

    def join(c, _):
        prefix[c] = jnp.dot(prefix[c - 1], fmaps[c], precision=HIGHEST)
        prefix_shift[c] = jnp.dot(prefix_shift[c - 1], fmaps[c], precision=HIGHEST) + shifts[c]
        return 0

    lax.fori_loop(1, chunks, join, 0)

    def smoother_unit(u, _):
        j, g = 1 + u // groups, lax.rem(u, groups)
        for k in range(GROUP):
            c = g * GROUP + k
            smaps[c] = sgain * propagate(smaps[c], diagonals[c, pl.ds(j, 1), :], rest_high[c, j], rest_low[c, j])
        return 0

    units = (length - 1) * groups
    before = jnp.minimum(units, (me * pace) // 8)
    lax.fori_loop(0, before, smoother_unit, 0)

    ends = (me == 0) | (me == count - 1)

    @pl.when(ends)
    def _():
        pl.semaphore_wait(barrier, 1)

    @pl.when(jnp.logical_not(ends))
    def _():
        pl.semaphore_wait(barrier, 2)

    def forward_copy(peer):
        return pltpu.make_async_remote_copy(
            src_ref=out_f, dst_ref=in_f, send_sem=send_sem.at[0], recv_sem=recv_sem.at[0], device_id={"tm": peer})

    def backward_copy(peer):
        return pltpu.make_async_remote_copy(
            src_ref=out_s, dst_ref=in_s, send_sem=send_sem.at[1], recv_sem=recv_sem.at[1], device_id={"tm": peer})

    start_row = jnp.broadcast_to(prior_ref[...], (SUB, width))

    @pl.when(me > 0)
    def _():
        forward_copy(me - 1).wait_recv()
        filtered[0] = in_f[...]

    @pl.when(me == 0)
    def _():
        filtered[0] = start_row

    start = filtered[0]
    column = to_column(start)[:, 0:1]

    @pl.when(me < count - 1)
    def _():
        moved = jnp.sum(prefix[chunks - 1] * column, axis=0, keepdims=True)
        out_f[...] = jnp.broadcast_to(moved, (SUB, width)) + prefix_shift[chunks - 1, 0:SUB, :]
        forward_copy(me + 1).start()

    lax.fori_loop(before, units, smoother_unit, 0)

    rows = [start[0:1]]
    for c in range(chunks - 1):
        rows.append(prefix_shift[c, 0:1, :] + jnp.sum(prefix[c] * column, axis=0, keepdims=True))
    states = jnp.concatenate(rows, axis=0)
    spot = lax.broadcasted_iota(jnp.int32, (width, LANES), 1)

    def forward(j, state):
        gathered = jnp.zeros((width, LANES), f32)
        for c in range(chunks):
            moved = jnp.sum(dense[c, j] * state[c:c + 1, :], axis=1, keepdims=True)
            gathered = jnp.where(spot == c, moved, gathered)
        predict = gathered.T[0:chunks]
        new = (1.0 - gains[j]) * predict + drives[j]
        filtered[j] = new
        change[j] = new - predict
        return new

    lax.fori_loop(0, length, forward, states)

    prefix[0] = smaps[0]

    def join_smoother(c, _):
        prefix[0] = jnp.dot(prefix[0], smaps[c], precision=HIGHEST)
        return 0

    lax.fori_loop(1, chunks, join_smoother, 0)

    def turned_step(j, values):
        columns = to_column(values)
        return jnp.concatenate([
            jnp.sum(dense[c, j] * columns[:, c:c + 1], axis=0, keepdims=True) for c in range(chunks)
        ], axis=0)

    def backward(i, carried):
        j = length - 1 - i
        return turned_step(j, change[j] + sgain * carried)

    carried = lax.fori_loop(0, length, backward, jnp.zeros((chunks, width), f32))

    def lowered(table, row):
        moved = jnp.sum(table * row, axis=1, keepdims=True)
        return jnp.broadcast_to(moved, (width, LANES)).T[0:1]

    shift = carried[chunks - 1:chunks]
    for c in range(chunks - 2, -1, -1):
        shift = carried[c:c + 1] + lowered(smaps[c], shift)

    @pl.when(me < count - 1)
    def _():
        backward_copy(me + 1).wait_recv()

    @pl.when(me == count - 1)
    def _():
        in_s[...] = jnp.zeros_like(in_s)

    entering = in_s[0:1, :]

    @pl.when(me > 0)
    def _():
        out_s[...] = jnp.broadcast_to(shift + lowered(prefix[0], entering), (SUB, width))
        backward_copy(me - 1).start()

    rows = [entering]
    for c in range(chunks - 1, 0, -1):
        rows.insert(0, carried[c:c + 1] + lowered(smaps[c], rows[0]))

    def final(i, carry):
        j = length - 1 - i
        lifted = sgain * carry
        smoothed = filtered[j] + lifted
        for c in range(chunks):
            smoothed_ref[0, pl.ds(c * length + j, 1), :] = smoothed[c:c + 1]
        residual = change[j] + lifted
        filtered[j] = residual
        return turned_step(j, residual)

    lax.fori_loop(0, length, final, jnp.concatenate(rows, axis=0))
    every = filtered[...].reshape(length * chunks, width)
    info_ref[...] = lax.dot_general(
        every, every, (((0,), (0,)), ((), ())), precision=HIGHEST, preferred_element_type=f32)

    @pl.when(me < count - 1)
    def _():
        forward_copy(me + 1).wait_send()

    @pl.when(me > 0)
    def _():
        backward_copy(me - 1).wait_send()


def total_kernel(parts, blocks, scale, local_ref, out_ref, part, box_e, box_t, send_sem, recv_sem):
    e, t = lax.axis_index("exp"), lax.axis_index("tm")
    barrier = pltpu.get_barrier_semaphore()
    e_peers = [lax.rem(e + k, parts) for k in range(1, parts)]
    t_peers = [lax.rem(t + k, blocks) for k in range(1, blocks)]
    for peer in e_peers:
        pl.semaphore_signal(barrier, inc=1, device_id={"exp": peer})
    for peer in t_peers:
        pl.semaphore_signal(barrier, inc=1, device_id={"tm": peer})
    pl.semaphore_wait(barrier, parts + blocks - 2)

    def send(src, dst, number, device):
        copy = pltpu.make_async_remote_copy(
            src_ref=src, dst_ref=dst, send_sem=send_sem.at[number], recv_sem=recv_sem.at[number],
            device_id=device)
        copy.start()
        return copy

    first = [send(local_ref.at[p], box_e.at[k], k, {"exp": p}) for k, p in enumerate(e_peers)]
    base = len(first)
    value = local_ref[e]
    for k, copy in enumerate(first):
        copy.wait_recv()
        value = value + box_e[k]
    part[...] = value
    second = [send(part.at[p], box_t.at[k], base + k, {"tm": p}) for k, p in enumerate(t_peers)]
    base += len(second)
    mine = part[t]
    for k, copy in enumerate(second):
        copy.wait_recv()
        mine = mine + box_t[k]
    out_ref[e, t] = mine * scale
    third = [send(out_ref.at[e, t], out_ref.at[e, t], base + k, {"tm": p}) for k, p in enumerate(t_peers)]
    base += len(third)
    for k, copy in enumerate(third):
        sender = lax.rem(t + blocks - 1 - k, blocks)
        pltpu.make_async_remote_copy(
            src_ref=out_ref.at[e, sender], dst_ref=out_ref.at[e, sender], send_sem=send_sem.at[base - len(third) + k],
            recv_sem=recv_sem.at[base - len(third) + k], device_id={"tm": sender}).wait_recv()
    fourth = [send(out_ref.at[e], out_ref.at[e], base + k, {"exp": p}) for k, p in enumerate(e_peers)]
    for k, copy in enumerate(fourth):
        sender = lax.rem(e + parts - 1 - k, parts)
        pltpu.make_async_remote_copy(
            src_ref=out_ref.at[sender], dst_ref=out_ref.at[sender], send_sem=send_sem.at[base + k],
            recv_sem=recv_sem.at[base + k], device_id={"exp": sender}).wait_recv()
    for copy in first + second + third + fourth:
        copy.wait_send()


def total(local, scale, ident):
    parts, blocks = lax.axis_size("exp"), lax.axis_size("tm")
    width = local.shape[0]
    rows = width // (parts * blocks)
    copies = 2 * (parts - 1) + 2 * (blocks - 1)
    f32 = jnp.float32
    vmem = pl.BlockSpec(memory_space=pltpu.VMEM)
    summed = pl.pallas_call(
        functools.partial(total_kernel, parts, blocks, scale),
        in_specs=[vmem],
        out_specs=vmem,
        out_shape=jax.ShapeDtypeStruct((parts, blocks, rows, width), f32),
        scratch_shapes=[
            pltpu.VMEM((blocks, rows, width), f32),
            pltpu.VMEM((parts - 1, blocks, rows, width), f32),
            pltpu.VMEM((blocks - 1, rows, width), f32),
            pltpu.SemaphoreType.DMA((copies,)),
            pltpu.SemaphoreType.DMA((copies,)),
        ],
        compiler_params=pltpu.CompilerParams(collective_id=ident, has_side_effects=True),
    )(local.reshape(parts, blocks, rows, width))
    return summed.reshape(width, width)


def shards(transitions, pattern, obs_mask, measured, prior_mean, filter_gain, smooth_gain):
    steps, width, _ = transitions.shape
    length = steps // CHUNKS
    f32 = jnp.float32
    vmem = pl.BlockSpec(memory_space=pltpu.VMEM)
    row = pltpu.VMEM((SUB, width), f32)
    square = (CHUNKS, width, width)
    by_step = pltpu.VMEM((length, CHUNKS, width), f32)
    smoothed, local_info = pl.pallas_call(
        functools.partial(estimate_kernel, lax.axis_size("tm"), PACE),
        in_specs=[pl.BlockSpec(memory_space=pltpu.SMEM), pl.BlockSpec(memory_space=pl.ANY)] + [vmem] * 5,
        out_specs=[vmem] * 2,
        out_shape=[jax.ShapeDtypeStruct((1, steps, width), f32), jax.ShapeDtypeStruct((width, width), f32)],
        scratch_shapes=[
            pltpu.VMEM((CHUNKS, length, width, width), f32),
            pltpu.VMEM((CHUNKS, length, width, width), jnp.bfloat16),
            pltpu.VMEM((CHUNKS, length, width, width), jnp.bfloat16),
            pltpu.VMEM((CHUNKS, length, width), f32),
            by_step,
            by_step,
            pltpu.VMEM(square, f32),
            pltpu.VMEM((CHUNKS, 2 * SUB, width), f32),
            pltpu.VMEM(square, f32),
            pltpu.VMEM(square, f32),
            pltpu.VMEM((CHUNKS, 2 * SUB, width), f32),
            by_step,
            by_step,
            row, row, row, row,
            pltpu.SemaphoreType.DMA((length,)),
            pltpu.SemaphoreType.DMA((2,)),
            pltpu.SemaphoreType.DMA((2,)),
        ],
        compiler_params=pltpu.CompilerParams(
            vmem_limit_bytes=VMEM_BYTES, collective_id=0, has_side_effects=True),
    )(pattern, transitions.reshape(CHUNKS, length, width, width), obs_mask, measured,
      filter_gain[None, :], smooth_gain[None, :], prior_mean)
    scale = 1.0 / (steps * lax.axis_size("tm") * lax.axis_size("exp"))
    return smoothed, total(local_info, scale, 1)


def solution(mesh):
    in_specs = (
        P("tm", None, None),
        P("tm", None, None),
        P("exp", "tm", None),
        P("exp", "tm", None),
        P("exp", None),
        P(),
        P(),
    )
    out_specs = (P("exp", "tm", None), P())
    return jax.shard_map(shards, mesh=mesh, in_specs=in_specs, out_specs=out_specs, check_vma=False)
```

```python
import functools

import jax
import jax.numpy as jnp
from jax import lax
from jax.experimental import pallas as pl
from jax.experimental.pallas import tpu as pltpu
from jax.sharding import PartitionSpec as P

HIGHEST = lax.Precision.HIGHEST
LANES = 128
SUB = 8
CHUNKS = 8
GROUP = 4
PACE = 16
VMEM_BYTES = 60 * 1024 * 1024


def split(x):
    high = x.astype(jnp.bfloat16)
    low = (x - high.astype(jnp.float32)).astype(jnp.bfloat16)
    return high, low


def dot_rhs_t(a, b):
    return lax.dot_general(a, b, (((1,), (1,)), ((), ())), preferred_element_type=jnp.float32)


def to_column(row):
    width = row.shape[1]
    padded = jnp.concatenate([row, jnp.zeros((LANES - SUB, width), jnp.float32)], axis=0)
    return padded.T


def estimate_kernel(parts, count, pace, scale, pattern_ref, trans_ref, obs_ref, meas_ref, fgain_ref, sgain_ref, prior_ref,
                    smoothed_ref, info_ref,
                    dense, rest_high, rest_low, diagonals, gains, drives, fmaps, shifts, smaps, prefix, prefix_shift,
                    filtered, change, out_f, in_f, out_s, in_s, local, part, box_e, box_t,
                    whole_map, load_sem, send_sem, recv_sem, total_send, total_recv):
    me = lax.axis_index("tm")
    chunks, length, width, _ = dense.shape
    blocks = pattern_ref.shape[1]
    block = width // blocks
    groups = chunks // GROUP
    f32 = jnp.float32
    barrier = pltpu.get_barrier_semaphore()

    part_at = lax.axis_index("exp")
    e_peers = [lax.rem(part_at + k, parts) for k in range(1, parts)]
    t_peers = [lax.rem(me + k, count) for k in range(1, count)]
    for peer in e_peers:
        pl.semaphore_signal(barrier, inc=1, device_id={"exp": peer})
    for peer in t_peers:
        pl.semaphore_signal(barrier, inc=1, device_id={"tm": peer})

    def load(j):
        return pltpu.make_async_copy(trans_ref.at[:, j], dense.at[:, j], load_sem.at[j])

    for j in range(length):
        load(j).start()
    fgain, sgain = fgain_ref[...], sgain_ref[...]
    lane = lax.broadcasted_iota(jnp.int32, (1, width), 1) // block
    on_diagonal = (lax.broadcasted_iota(jnp.int32, (width, width), 0)
                   == lax.broadcasted_iota(jnp.int32, (width, width), 1))

    def gains_of(c, j):
        t = c * length + j
        gain = fgain * obs_ref[0, pl.ds(t, 1), :].astype(f32)
        drive = gain * meas_ref[0, pl.ds(t, 1), :]
        gains[j, pl.ds(c, 1), :] = gain
        drives[j, pl.ds(c, 1), :] = drive
        return 1.0 - gain, drive

    def masked(c, j):
        t = c * length + j
        pieces = []
        for i in range(blocks):
            weights = jnp.zeros((1, width), f32)
            for k in range(blocks):
                weights = jnp.where(lane == k, pattern_ref[t, i, k].astype(f32), weights)
            pieces.append(dense[c, j, i * block:(i + 1) * block, :] * weights)
        value = jnp.concatenate(pieces, axis=0)
        dense[c, j] = value
        return value

    def propagate(rows, diagonal, right_high, right_low):
        high, low = split(rows)
        left = jnp.concatenate([high, low, high], axis=1)
        right = jnp.concatenate([right_high, right_high, right_low], axis=1)
        return rows * diagonal + dot_rhs_t(left, right)

    load(0).wait()

    def first_step(c, _):
        keep, drive = gains_of(c, 0)
        turned = masked(c, 0).T
        fmaps[c] = turned * keep
        smaps[c] = turned * sgain
        shifts[c] = jnp.broadcast_to(drive, (2 * SUB, width))
        return 0

    lax.fori_loop(0, chunks, first_step, 0)

    def filter_step(j, _):
        load(j).wait()

        def group_step(g, _):
            for k in range(GROUP):
                c = g * GROUP + k
                keep, drive = gains_of(c, j)
                value = masked(c, j)
                diagonal = jnp.sum(jnp.where(on_diagonal, value, 0.0), axis=0, keepdims=True)
                high, low = split(jnp.where(on_diagonal, 0.0, value))
                diagonals[c, pl.ds(j, 1), :] = diagonal
                rest_high[c, j] = high
                rest_low[c, j] = low
                moved = propagate(jnp.concatenate([fmaps[c], shifts[c]], axis=0), diagonal, high, low)
                fmaps[c] = moved[0:width] * keep
                shifts[c] = moved[width:] * keep + drive
            return 0

        return lax.fori_loop(0, groups, group_step, 0)

    lax.fori_loop(1, length, filter_step, 0)

    prefix[0] = fmaps[0]
    prefix_shift[0] = shifts[0]

    def join(c, _):
        prefix[c] = jnp.dot(prefix[c - 1], fmaps[c], precision=HIGHEST)
        prefix_shift[c] = jnp.dot(prefix_shift[c - 1], fmaps[c], precision=HIGHEST) + shifts[c]
        return 0

    lax.fori_loop(1, chunks, join, 0)

    def smoother_unit(u, _):
        j, g = 1 + u // groups, lax.rem(u, groups)
        for k in range(GROUP):
            c = g * GROUP + k
            smaps[c] = sgain * propagate(smaps[c], diagonals[c, pl.ds(j, 1), :], rest_high[c, j], rest_low[c, j])
        return 0

    units = (length - 1) * groups
    before = jnp.minimum(units, (me * pace) // 8)
    lax.fori_loop(0, before, smoother_unit, 0)

    def join_smoother(c, _):
        whole_map[...] = jnp.dot(whole_map[...], smaps[c], precision=HIGHEST)
        return 0

    def join_all():
        whole_map[...] = smaps[0]
        lax.fori_loop(1, chunks, join_smoother, 0)

    early = before == units

    @pl.when(early)
    def _():
        join_all()

    pl.semaphore_wait(barrier, parts + count - 2)

    def forward_copy(peer):
        return pltpu.make_async_remote_copy(
            src_ref=out_f, dst_ref=in_f, send_sem=send_sem.at[0], recv_sem=recv_sem.at[0], device_id={"tm": peer})

    def backward_copy(peer):
        return pltpu.make_async_remote_copy(
            src_ref=out_s, dst_ref=in_s, send_sem=send_sem.at[1], recv_sem=recv_sem.at[1], device_id={"tm": peer})

    start_row = jnp.broadcast_to(prior_ref[...], (SUB, width))

    @pl.when(me > 0)
    def _():
        forward_copy(me - 1).wait_recv()
        filtered[0] = in_f[...]

    @pl.when(me == 0)
    def _():
        filtered[0] = start_row

    start = filtered[0]
    column = to_column(start)[:, 0:1]

    @pl.when(me < count - 1)
    def _():
        moved = jnp.sum(prefix[chunks - 1] * column, axis=0, keepdims=True)
        out_f[...] = jnp.broadcast_to(moved, (SUB, width)) + prefix_shift[chunks - 1, 0:SUB, :]
        forward_copy(me + 1).start()

    lax.fori_loop(before, units, smoother_unit, 0)

    rows = [start[0:1]]
    for c in range(chunks - 1):
        rows.append(prefix_shift[c, 0:1, :] + jnp.sum(prefix[c] * column, axis=0, keepdims=True))
    states = jnp.concatenate(rows, axis=0)
    spot = lax.broadcasted_iota(jnp.int32, (width, LANES), 1)

    def forward(j, state):
        gathered = jnp.zeros((width, LANES), f32)
        for c in range(chunks):
            moved = jnp.sum(dense[c, j] * state[c:c + 1, :], axis=1, keepdims=True)
            gathered = jnp.where(spot == c, moved, gathered)
        predict = gathered.T[0:chunks]
        new = (1.0 - gains[j]) * predict + drives[j]
        filtered[j] = new
        change[j] = new - predict
        return new

    lax.fori_loop(0, length, forward, states)

    @pl.when(jnp.logical_not(early))
    def _():
        join_all()

    def turned_step(j, values):
        columns = to_column(values)
        return jnp.concatenate([
            jnp.sum(dense[c, j] * columns[:, c:c + 1], axis=0, keepdims=True) for c in range(chunks)
        ], axis=0)

    def backward(i, carried):
        j = length - 1 - i
        return turned_step(j, change[j] + sgain * carried)

    carried = lax.fori_loop(0, length, backward, jnp.zeros((chunks, width), f32))

    def lowered(table, row):
        moved = jnp.sum(table * row, axis=1, keepdims=True)
        return jnp.broadcast_to(moved, (width, LANES)).T[0:1]

    shift = carried[chunks - 1:chunks]
    for c in range(chunks - 2, -1, -1):
        shift = carried[c:c + 1] + lowered(smaps[c], shift)

    @pl.when(me < count - 1)
    def _():
        backward_copy(me + 1).wait_recv()

    @pl.when(me == count - 1)
    def _():
        in_s[...] = jnp.zeros_like(in_s)

    entering = in_s[0:1, :]

    @pl.when(me > 0)
    def _():
        out_s[...] = jnp.broadcast_to(shift + lowered(whole_map[...], entering), (SUB, width))
        backward_copy(me - 1).start()

    rows = [entering]
    for c in range(chunks - 1, 0, -1):
        rows.insert(0, carried[c:c + 1] + lowered(smaps[c], rows[0]))

    def final(i, carry):
        j = length - 1 - i
        lifted = sgain * carry
        smoothed = filtered[j] + lifted
        for c in range(chunks):
            smoothed_ref[0, pl.ds(c * length + j, 1), :] = smoothed[c:c + 1]
        residual = change[j] + lifted
        filtered[j] = residual
        return turned_step(j, residual)

    lax.fori_loop(0, length, final, jnp.concatenate(rows, axis=0))
    every = filtered[...].reshape(length * chunks, width)
    local[...] = lax.dot_general(
        every, every, (((0,), (0,)), ((), ())), precision=HIGHEST, preferred_element_type=f32,
    ).reshape(local.shape)
    add_up(part_at, me, e_peers, t_peers, scale, local, info_ref, part, box_e, box_t, total_send, total_recv)

    @pl.when(me < count - 1)
    def _():
        forward_copy(me + 1).wait_send()

    @pl.when(me > 0)
    def _():
        backward_copy(me - 1).wait_send()


def add_up(e, t, e_peers, t_peers, scale, local_ref, out_ref, part, box_e, box_t, send_sem, recv_sem):
    parts, blocks = len(e_peers) + 1, len(t_peers) + 1

    def send(src, dst, number, device):
        copy = pltpu.make_async_remote_copy(
            src_ref=src, dst_ref=dst, send_sem=send_sem.at[number], recv_sem=recv_sem.at[number],
            device_id=device)
        copy.start()
        return copy

    first = [send(local_ref.at[p], box_e.at[k], k, {"exp": p}) for k, p in enumerate(e_peers)]
    base = len(first)
    value = local_ref[e]
    for k, copy in enumerate(first):
        copy.wait_recv()
        value = value + box_e[k]
    part[...] = value
    second = [send(part.at[p], box_t.at[k], base + k, {"tm": p}) for k, p in enumerate(t_peers)]
    base += len(second)
    mine = part[t]
    for k, copy in enumerate(second):
        copy.wait_recv()
        mine = mine + box_t[k]
    out_ref[e, t] = mine * scale
    third = [send(out_ref.at[e, t], out_ref.at[e, t], base + k, {"tm": p}) for k, p in enumerate(t_peers)]
    base += len(third)
    for k, copy in enumerate(third):
        sender = lax.rem(t + blocks - 1 - k, blocks)
        pltpu.make_async_remote_copy(
            src_ref=out_ref.at[e, sender], dst_ref=out_ref.at[e, sender], send_sem=send_sem.at[base - len(third) + k],
            recv_sem=recv_sem.at[base - len(third) + k], device_id={"tm": sender}).wait_recv()
    fourth = [send(out_ref.at[e], out_ref.at[e], base + k, {"exp": p}) for k, p in enumerate(e_peers)]
    for k, copy in enumerate(fourth):
        sender = lax.rem(e + parts - 1 - k, parts)
        pltpu.make_async_remote_copy(
            src_ref=out_ref.at[sender], dst_ref=out_ref.at[sender], send_sem=send_sem.at[base + k],
            recv_sem=recv_sem.at[base + k], device_id={"exp": sender}).wait_recv()
    for copy in first + second + third + fourth:
        copy.wait_send()


def shards(transitions, pattern, obs_mask, measured, prior_mean, filter_gain, smooth_gain):
    steps, width, _ = transitions.shape
    length = steps // CHUNKS
    f32 = jnp.float32
    vmem = pl.BlockSpec(memory_space=pltpu.VMEM)
    row = pltpu.VMEM((SUB, width), f32)
    square = (CHUNKS, width, width)
    by_step = pltpu.VMEM((length, CHUNKS, width), f32)
    parts, blocks = lax.axis_size("exp"), lax.axis_size("tm")
    rows = width // (parts * blocks)
    scale = 1.0 / (steps * blocks * parts)
    copies = 2 * (parts + blocks - 2)
    smoothed, information = pl.pallas_call(
        functools.partial(estimate_kernel, parts, blocks, PACE, scale),
        in_specs=[pl.BlockSpec(memory_space=pltpu.SMEM), pl.BlockSpec(memory_space=pl.ANY)] + [vmem] * 5,
        out_specs=[vmem] * 2,
        out_shape=[jax.ShapeDtypeStruct((1, steps, width), f32), jax.ShapeDtypeStruct((parts, blocks, rows, width), f32)],
        scratch_shapes=[
            pltpu.VMEM((CHUNKS, length, width, width), f32),
            pltpu.VMEM((CHUNKS, length, width, width), jnp.bfloat16),
            pltpu.VMEM((CHUNKS, length, width, width), jnp.bfloat16),
            pltpu.VMEM((CHUNKS, length, width), f32),
            by_step,
            by_step,
            pltpu.VMEM(square, f32),
            pltpu.VMEM((CHUNKS, 2 * SUB, width), f32),
            pltpu.VMEM(square, f32),
            pltpu.VMEM(square, f32),
            pltpu.VMEM((CHUNKS, 2 * SUB, width), f32),
            by_step,
            by_step,
            row, row, row, row,
            pltpu.VMEM((parts, blocks, rows, width), f32),
            pltpu.VMEM((blocks, rows, width), f32),
            pltpu.VMEM((parts - 1, blocks, rows, width), f32),
            pltpu.VMEM((blocks - 1, rows, width), f32),
            pltpu.VMEM((width, width), f32),
            pltpu.SemaphoreType.DMA((length,)),
            pltpu.SemaphoreType.DMA((2,)),
            pltpu.SemaphoreType.DMA((2,)),
            pltpu.SemaphoreType.DMA((copies,)),
            pltpu.SemaphoreType.DMA((copies,)),
        ],
        compiler_params=pltpu.CompilerParams(
            vmem_limit_bytes=VMEM_BYTES, collective_id=0, has_side_effects=True),
    )(pattern, transitions.reshape(CHUNKS, length, width, width), obs_mask, measured,
      filter_gain[None, :], smooth_gain[None, :], prior_mean)
    return smoothed, information.reshape(width, width)


def solution(mesh):
    in_specs = (
        P("tm", None, None),
        P("tm", None, None),
        P("exp", "tm", None),
        P("exp", "tm", None),
        P("exp", None),
        P(),
        P(),
    )
    out_specs = (P("exp", "tm", None), P())
    return jax.shard_map(shards, mesh=mesh, in_specs=in_specs, out_specs=out_specs, check_vma=False)
```

```python
import functools

import jax
import jax.numpy as jnp
from jax import lax
from jax.experimental import pallas as pl
from jax.experimental.pallas import tpu as pltpu
from jax.sharding import PartitionSpec as P

HIGHEST = lax.Precision.HIGHEST
LANES = 128
SUB = 8
CHUNKS = 8
GROUP = 8
PACE = 16
VMEM_BYTES = 60 * 1024 * 1024


def split(x):
    high = x.astype(jnp.bfloat16)
    low = (x - high.astype(jnp.float32)).astype(jnp.bfloat16)
    return high, low


def dot_rhs_t(a, b):
    return lax.dot_general(a, b, (((1,), (1,)), ((), ())), preferred_element_type=jnp.float32)


def to_column(row):
    width = row.shape[1]
    padded = jnp.concatenate([row, jnp.zeros((LANES - SUB, width), jnp.float32)], axis=0)
    return padded.T


def estimate_kernel(parts, count, pace, scale, pattern_ref, trans_ref, obs_ref, meas_ref, fgain_ref, sgain_ref, prior_ref,
                    smoothed_ref, info_ref,
                    dense, rest_high, rest_low, diagonals, gains, drives, fmaps, shifts, smaps, prefix, prefix_shift,
                    filtered, change, out_f, in_f, out_s, in_s, local, part, box_e, box_t,
                    whole_map, load_sem, send_sem, recv_sem, total_send, total_recv):
    me = lax.axis_index("tm")
    chunks, length, width, _ = dense.shape
    blocks = pattern_ref.shape[1]
    block = width // blocks
    groups = chunks // GROUP
    f32 = jnp.float32
    barrier = pltpu.get_barrier_semaphore()

    part_at = lax.axis_index("exp")
    e_peers = [lax.rem(part_at + k, parts) for k in range(1, parts)]
    t_peers = [lax.rem(me + k, count) for k in range(1, count)]
    for peer in e_peers:
        pl.semaphore_signal(barrier, inc=1, device_id={"exp": peer})
    for peer in t_peers:
        pl.semaphore_signal(barrier, inc=1, device_id={"tm": peer})

    def load(j):
        return pltpu.make_async_copy(trans_ref.at[:, j], dense.at[:, j], load_sem.at[j])

    for j in range(length):
        load(j).start()
    fgain, sgain = fgain_ref[...], sgain_ref[...]
    lane = lax.broadcasted_iota(jnp.int32, (1, width), 1) // block
    on_diagonal = (lax.broadcasted_iota(jnp.int32, (width, width), 0)
                   == lax.broadcasted_iota(jnp.int32, (width, width), 1))

    def gains_of(c, j):
        t = c * length + j
        gain = fgain * obs_ref[0, pl.ds(t, 1), :].astype(f32)
        drive = gain * meas_ref[0, pl.ds(t, 1), :]
        gains[j, pl.ds(c, 1), :] = gain
        drives[j, pl.ds(c, 1), :] = drive
        return 1.0 - gain, drive

    def masked(c, j):
        t = c * length + j
        pieces = []
        for i in range(blocks):
            weights = jnp.zeros((1, width), f32)
            for k in range(blocks):
                weights = jnp.where(lane == k, pattern_ref[t, i, k].astype(f32), weights)
            pieces.append(dense[c, j, i * block:(i + 1) * block, :] * weights)
        value = jnp.concatenate(pieces, axis=0)
        dense[c, j] = value
        return value

    def propagate(rows, diagonal, right_high, right_low):
        high, low = split(rows)
        left = jnp.concatenate([high, low, high], axis=1)
        right = jnp.concatenate([right_high, right_high, right_low], axis=1)
        return rows * diagonal + dot_rhs_t(left, right)

    load(0).wait()

    def first_step(c, _):
        keep, drive = gains_of(c, 0)
        turned = masked(c, 0).T
        fmaps[c] = turned * keep
        smaps[c] = turned * sgain
        shifts[c] = jnp.broadcast_to(drive, (2 * SUB, width))
        return 0

    lax.fori_loop(0, chunks, first_step, 0)

    def filter_step(j, _):
        load(j).wait()

        def group_step(g, _):
            for k in range(GROUP):
                c = g * GROUP + k
                keep, drive = gains_of(c, j)
                value = masked(c, j)
                diagonal = jnp.sum(jnp.where(on_diagonal, value, 0.0), axis=0, keepdims=True)
                high, low = split(jnp.where(on_diagonal, 0.0, value))
                diagonals[c, pl.ds(j, 1), :] = diagonal
                rest_high[c, j] = high
                rest_low[c, j] = low
                moved = propagate(jnp.concatenate([fmaps[c], shifts[c]], axis=0), diagonal, high, low)
                fmaps[c] = moved[0:width] * keep
                shifts[c] = moved[width:] * keep + drive
            return 0

        return lax.fori_loop(0, groups, group_step, 0)

    lax.fori_loop(1, length, filter_step, 0)

    prefix[0] = fmaps[0]
    prefix_shift[0] = shifts[0]

    def join(c, _):
        prefix[c] = jnp.dot(prefix[c - 1], fmaps[c], precision=HIGHEST)
        prefix_shift[c] = jnp.dot(prefix_shift[c - 1], fmaps[c], precision=HIGHEST) + shifts[c]
        return 0

    lax.fori_loop(1, chunks, join, 0)

    def smoother_unit(u, _):
        j, g = 1 + u // groups, lax.rem(u, groups)
        for k in range(GROUP):
            c = g * GROUP + k
            smaps[c] = sgain * propagate(smaps[c], diagonals[c, pl.ds(j, 1), :], rest_high[c, j], rest_low[c, j])
        return 0

    units = (length - 1) * groups
    before = jnp.minimum(units, (me * pace) // 8)
    lax.fori_loop(0, before, smoother_unit, 0)

    def join_smoother(c, _):
        whole_map[...] = jnp.dot(whole_map[...], smaps[c], precision=HIGHEST)
        return 0

    def join_all():
        whole_map[...] = smaps[0]
        lax.fori_loop(1, chunks, join_smoother, 0)

    early = before == units

    @pl.when(early)
    def _():
        join_all()

    pl.semaphore_wait(barrier, parts + count - 2)

    def forward_copy(peer):
        return pltpu.make_async_remote_copy(
            src_ref=out_f, dst_ref=in_f, send_sem=send_sem.at[0], recv_sem=recv_sem.at[0], device_id={"tm": peer})

    def backward_copy(peer):
        return pltpu.make_async_remote_copy(
            src_ref=out_s, dst_ref=in_s, send_sem=send_sem.at[1], recv_sem=recv_sem.at[1], device_id={"tm": peer})

    start_row = jnp.broadcast_to(prior_ref[...], (SUB, width))

    @pl.when(me > 0)
    def _():
        forward_copy(me - 1).wait_recv()
        filtered[0] = in_f[...]

    @pl.when(me == 0)
    def _():
        filtered[0] = start_row

    start = filtered[0]
    column = to_column(start)[:, 0:1]

    @pl.when(me < count - 1)
    def _():
        moved = jnp.sum(prefix[chunks - 1] * column, axis=0, keepdims=True)
        out_f[...] = jnp.broadcast_to(moved, (SUB, width)) + prefix_shift[chunks - 1, 0:SUB, :]
        forward_copy(me + 1).start()

    lax.fori_loop(before, units, smoother_unit, 0)

    rows = [start[0:1]]
    for c in range(chunks - 1):
        rows.append(prefix_shift[c, 0:1, :] + jnp.sum(prefix[c] * column, axis=0, keepdims=True))
    states = jnp.concatenate(rows, axis=0)
    spot = lax.broadcasted_iota(jnp.int32, (width, LANES), 1)

    def forward(j, state):
        gathered = jnp.zeros((width, LANES), f32)
        for c in range(chunks):
            moved = jnp.sum(dense[c, j] * state[c:c + 1, :], axis=1, keepdims=True)
            gathered = jnp.where(spot == c, moved, gathered)
        predict = gathered.T[0:chunks]
        new = (1.0 - gains[j]) * predict + drives[j]
        filtered[j] = new
        change[j] = new - predict
        return new

    lax.fori_loop(0, length, forward, states)

    @pl.when(jnp.logical_not(early))
    def _():
        join_all()

    def turned_step(j, values):
        columns = to_column(values)
        return jnp.concatenate([
            jnp.sum(dense[c, j] * columns[:, c:c + 1], axis=0, keepdims=True) for c in range(chunks)
        ], axis=0)

    def backward(i, carried):
        j = length - 1 - i
        return turned_step(j, change[j] + sgain * carried)

    carried = lax.fori_loop(0, length, backward, jnp.zeros((chunks, width), f32))

    def lowered(table, row):
        moved = jnp.sum(table * row, axis=1, keepdims=True)
        return jnp.broadcast_to(moved, (width, LANES)).T[0:1]

    shift = carried[chunks - 1:chunks]
    for c in range(chunks - 2, -1, -1):
        shift = carried[c:c + 1] + lowered(smaps[c], shift)

    @pl.when(me < count - 1)
    def _():
        backward_copy(me + 1).wait_recv()

    @pl.when(me == count - 1)
    def _():
        in_s[...] = jnp.zeros_like(in_s)

    entering = in_s[0:1, :]

    @pl.when(me > 0)
    def _():
        out_s[...] = jnp.broadcast_to(shift + lowered(whole_map[...], entering), (SUB, width))
        backward_copy(me - 1).start()

    rows = [entering]
    for c in range(chunks - 1, 0, -1):
        rows.insert(0, carried[c:c + 1] + lowered(smaps[c], rows[0]))

    def final(i, carry):
        j = length - 1 - i
        lifted = sgain * carry
        smoothed = filtered[j] + lifted
        for c in range(chunks):
            smoothed_ref[0, pl.ds(c * length + j, 1), :] = smoothed[c:c + 1]
        residual = change[j] + lifted
        filtered[j] = residual
        return turned_step(j, residual)

    lax.fori_loop(0, length, final, jnp.concatenate(rows, axis=0))
    every = filtered[...].reshape(length * chunks, width)
    local[...] = lax.dot_general(
        every, every, (((0,), (0,)), ((), ())), precision=HIGHEST, preferred_element_type=f32,
    ).reshape(local.shape)
    add_up(part_at, me, e_peers, t_peers, scale, local, info_ref, part, box_e, box_t, total_send, total_recv)

    @pl.when(me < count - 1)
    def _():
        forward_copy(me + 1).wait_send()

    @pl.when(me > 0)
    def _():
        backward_copy(me - 1).wait_send()


def add_up(e, t, e_peers, t_peers, scale, local_ref, out_ref, part, box_e, box_t, send_sem, recv_sem):
    parts, blocks = len(e_peers) + 1, len(t_peers) + 1

    def send(src, dst, number, device):
        copy = pltpu.make_async_remote_copy(
            src_ref=src, dst_ref=dst, send_sem=send_sem.at[number], recv_sem=recv_sem.at[number],
            device_id=device)
        copy.start()
        return copy

    first = [send(local_ref.at[p], box_e.at[k], k, {"exp": p}) for k, p in enumerate(e_peers)]
    base = len(first)
    value = local_ref[e]
    for k, copy in enumerate(first):
        copy.wait_recv()
        value = value + box_e[k]
    part[...] = value
    second = [send(part.at[p], box_t.at[k], base + k, {"tm": p}) for k, p in enumerate(t_peers)]
    base += len(second)
    mine = part[t]
    for k, copy in enumerate(second):
        copy.wait_recv()
        mine = mine + box_t[k]
    out_ref[e, t] = mine * scale
    third = [send(out_ref.at[e, t], out_ref.at[e, t], base + k, {"tm": p}) for k, p in enumerate(t_peers)]
    base += len(third)
    for k, copy in enumerate(third):
        sender = lax.rem(t + blocks - 1 - k, blocks)
        pltpu.make_async_remote_copy(
            src_ref=out_ref.at[e, sender], dst_ref=out_ref.at[e, sender], send_sem=send_sem.at[base - len(third) + k],
            recv_sem=recv_sem.at[base - len(third) + k], device_id={"tm": sender}).wait_recv()
    fourth = [send(out_ref.at[e], out_ref.at[e], base + k, {"exp": p}) for k, p in enumerate(e_peers)]
    for k, copy in enumerate(fourth):
        sender = lax.rem(e + parts - 1 - k, parts)
        pltpu.make_async_remote_copy(
            src_ref=out_ref.at[sender], dst_ref=out_ref.at[sender], send_sem=send_sem.at[base + k],
            recv_sem=recv_sem.at[base + k], device_id={"exp": sender}).wait_recv()
    for copy in first + second + third + fourth:
        copy.wait_send()


def shards(transitions, pattern, obs_mask, measured, prior_mean, filter_gain, smooth_gain):
    steps, width, _ = transitions.shape
    length = steps // CHUNKS
    f32 = jnp.float32
    vmem = pl.BlockSpec(memory_space=pltpu.VMEM)
    row = pltpu.VMEM((SUB, width), f32)
    square = (CHUNKS, width, width)
    by_step = pltpu.VMEM((length, CHUNKS, width), f32)
    parts, blocks = lax.axis_size("exp"), lax.axis_size("tm")
    rows = width // (parts * blocks)
    scale = 1.0 / (steps * blocks * parts)
    copies = 2 * (parts + blocks - 2)
    smoothed, information = pl.pallas_call(
        functools.partial(estimate_kernel, parts, blocks, PACE, scale),
        in_specs=[pl.BlockSpec(memory_space=pltpu.SMEM), pl.BlockSpec(memory_space=pl.ANY)] + [vmem] * 5,
        out_specs=[vmem] * 2,
        out_shape=[jax.ShapeDtypeStruct((1, steps, width), f32), jax.ShapeDtypeStruct((parts, blocks, rows, width), f32)],
        scratch_shapes=[
            pltpu.VMEM((CHUNKS, length, width, width), f32),
            pltpu.VMEM((CHUNKS, length, width, width), jnp.bfloat16),
            pltpu.VMEM((CHUNKS, length, width, width), jnp.bfloat16),
            pltpu.VMEM((CHUNKS, length, width), f32),
            by_step,
            by_step,
            pltpu.VMEM(square, f32),
            pltpu.VMEM((CHUNKS, 2 * SUB, width), f32),
            pltpu.VMEM(square, f32),
            pltpu.VMEM(square, f32),
            pltpu.VMEM((CHUNKS, 2 * SUB, width), f32),
            by_step,
            by_step,
            row, row, row, row,
            pltpu.VMEM((parts, blocks, rows, width), f32),
            pltpu.VMEM((blocks, rows, width), f32),
            pltpu.VMEM((parts - 1, blocks, rows, width), f32),
            pltpu.VMEM((blocks - 1, rows, width), f32),
            pltpu.VMEM((width, width), f32),
            pltpu.SemaphoreType.DMA((length,)),
            pltpu.SemaphoreType.DMA((2,)),
            pltpu.SemaphoreType.DMA((2,)),
            pltpu.SemaphoreType.DMA((copies,)),
            pltpu.SemaphoreType.DMA((copies,)),
        ],
        compiler_params=pltpu.CompilerParams(
            vmem_limit_bytes=VMEM_BYTES, collective_id=0, has_side_effects=True),
    )(pattern, transitions.reshape(CHUNKS, length, width, width), obs_mask, measured,
      filter_gain[None, :], smooth_gain[None, :], prior_mean)
    return smoothed, information.reshape(width, width)


def solution(mesh):
    in_specs = (
        P("tm", None, None),
        P("tm", None, None),
        P("exp", "tm", None),
        P("exp", "tm", None),
        P("exp", None),
        P(),
        P(),
    )
    out_specs = (P("exp", "tm", None), P())
    return jax.shard_map(shards, mesh=mesh, in_specs=in_specs, out_specs=out_specs, check_vma=False)
```
